512 devices in a mesh: mem: 2 (over core), tile: 256 (over z, y, x).
Axes of the slice: x: 4, y: 8, z: 8, core: 2. Of those that a mesh axis runs over, the one named last changes fastest.
Arguments:
- anomalies: bfloat16 [1024, 256, 512], P('tile', 'mem'), may hold values from -6 to 6
- innovations: bfloat16 [2048, 256, 512], P('tile', 'mem'), may hold values from -3 to 3
- obs_tile: int32 [2048], P('tile'), may hold values from 0 to 1023, as said below
- pair_tiles: int32 [2048, 2], P('tile'), may hold values from 0 to 1023, as said below
- loc_bin: int32 [2048], P('tile'), may hold values from 0 to 4
Outputs:
- analysis: bfloat16 [1024, 256, 512], P('tile', 'mem')
The draws below stay inside these ranges and needn't reach their ends.
Inputs may be any that keep to these rules, and one draw needn't show every extreme that they name: Block o lies in a tile of its own index of tile: obs_tile[o] // 4 == o // 8. `pair_tiles`: slot k's first tile i has i // 4 == k // 8; its second tile j differs from i and j // 4 - i // 4 lies in 0 to 2, equal to 2 for some slot. Pairs may repeat. `loc_bin`: bin 4 marks an empty slot.
All inputs are finite; a program needn't handle non-finite values.
Results may differ from the reference program's by a relative error of at most 0.0051.
Values may be sent and summed in bfloat16 or wider, within the bound.
A program may use at most 128 MiB of HBM per device.

```python
import jax
import jax.numpy as jnp
from jax import lax

MEMBERS = 256
POINTS = 512
TILE_DEV = 4
HOPS = 2
NBIN = 4
RADIUS = 4
PAIR_DEV = 8
OBS_DEV = 8
TILES = 1024
PAIRS = 2048
OBS = 2048


def draw_obs_tile(key, part):
    rows = jnp.arange(OBS, dtype=jnp.int32)
    device = rows // OBS_DEV
    local = jax.random.randint(key, (OBS,), 0, TILE_DEV, dtype=jnp.int32)
    local = jnp.where(rows % OBS_DEV == 0, TILE_DEV - 1, local)
    return device * TILE_DEV + local


def draw_pair_tiles(key, part):
    devices_all = TILES // TILE_DEV
    rows = jnp.arange(PAIRS, dtype=jnp.int32)
    device = rows // PAIR_DEV
    slot = rows % PAIR_DEV
    key_first, key_step, key_far, key_near = jax.random.split(key, 4)
    first_local = jax.random.randint(key_first, (PAIRS,), 0, TILE_DEV, dtype=jnp.int32)
    first_local = jnp.where(jnp.logical_and(device == devices_all - 1, slot == 1), TILE_DEV - 1, first_local)
    step = jax.random.randint(key_step, (PAIRS,), 0, HOPS + 1, dtype=jnp.int32)
    step = jnp.where(slot == 0, HOPS, step)
    step = jnp.where(device + step >= devices_all, 0, step)
    far_local = jax.random.randint(key_far, (PAIRS,), 0, TILE_DEV, dtype=jnp.int32)
    near_local = (first_local + 1 + jax.random.randint(key_near, (PAIRS,), 0, TILE_DEV - 1, dtype=jnp.int32)) % TILE_DEV
    second_local = jnp.where(step == 0, near_local, far_local)
    first = device * TILE_DEV + first_local
    second = (device + step) * TILE_DEV + second_local
    return jnp.stack([first, second], axis=1)


def place_ends(drawn, key, least, largest):
    dims = drawn.shape
    spot = [jax.random.randint(jax.random.fold_in(key, axis), (), 0, dims[axis]) for axis in range(len(dims))]
    drawn = drawn.at[tuple(spot)].set(least)
    longest = dims.index(max(dims))
    spot[longest] = (spot[longest] + 1) % dims[longest]
    return drawn.at[tuple(spot)].set(largest)


def block_scale(rng, dims, cuts, smallest, largest):
    factor_of, own = 1.0, jax.random.fold_in(rng, 6)
    for position, blocks in cuts:
        heights = jnp.exp(jax.random.uniform(jax.random.fold_in(own, position), (blocks,), jnp.float32, smallest / len(cuts), largest / len(cuts)))
        factor_of = factor_of * jnp.repeat(heights, dims[position] // blocks).reshape([-1 if axis == position else 1 for axis in range(len(dims))])
    return factor_of


def bell_draw(stream_key, extent, spread, limit, cuts=(), held_as=jnp.bfloat16):
    drawn = jax.random.normal(stream_key, extent, jnp.float32) * spread
    if len(cuts) > 0:
        drawn = block_scale(stream_key, extent, cuts, -0.22, 0.18) * drawn
    return jnp.clip(drawn, min=-limit, max=limit).astype(held_as)


def setup_inputs(seed: int = 0) -> dict:
    key_of = jax.random.split(jax.random.key(seed), 6)
    anomalies = bell_draw(key_of[0], (TILES, MEMBERS, POINTS), 1.0, 6.0, ((0, 256), (1, 2)))
    innovations = bell_draw(key_of[1], (OBS, MEMBERS, POINTS), 0.5, 3.0, ((0, 256), (1, 2)))
    obs_tile = draw_obs_tile(jax.random.fold_in(key_of[5], 71), 0)
    pair_tiles = draw_pair_tiles(jax.random.fold_in(key_of[5], 71), 0)
    loc_bin = place_ends(jax.random.randint(key_of[4], (PAIRS,), 0, NBIN + 1), jax.random.fold_in(key_of[4], 1), 0, NBIN).astype(jnp.int32)
    return dict(anomalies=anomalies, innovations=innovations, obs_tile=obs_tile, pair_tiles=pair_tiles, loc_bin=loc_bin)


def weights_for(bins, points):
    positions = jnp.arange(points, dtype=jnp.int32)
    column = (positions % 32).astype(jnp.float32)
    levels = (positions // 32).astype(jnp.float32)
    along = 0.5 * RADIUS * bins.astype(jnp.float32)[:, None, None] + column[None, None, :] - column[None, :, None]
    across = levels[None, None, :] - levels[None, :, None]
    weight = jnp.exp(-(along * along + across * across) / (2.0 * RADIUS * RADIUS))
    return jnp.where(bins[:, None, None] < NBIN, weight, 0.0)


def reference(anomalies, innovations, obs_tile, pair_tiles, loc_bin):
    tiles_all = anomalies.shape[0]
    points = anomalies.shape[2]
    onehot = (obs_tile[:, None] == jnp.arange(tiles_all, dtype=jnp.int32)[None, :]).astype(jnp.float32)
    forcing = jnp.einsum("ot,omp->tmp", onehot, innovations.astype(jnp.float32)).astype(jnp.bfloat16)
    zero_bin = weights_for(jnp.zeros((1,), jnp.int32), points)[0]

    def self_term(tile_index):
        block = anomalies[tile_index]
        cross = jnp.dot(block.T, block, preferred_element_type=jnp.float32)
        own = (zero_bin * cross / (MEMBERS - 1)).astype(jnp.bfloat16)
        return jnp.dot(forcing[tile_index], own.T, preferred_element_type=jnp.float32)

    increment = lax.map(self_term, jnp.arange(tiles_all, dtype=jnp.int32))

    def pair_step(total, slot):
        first = slot[0]
        second = slot[1]
        bin_value = slot[2]
        cross = jnp.dot(anomalies[first].T, anomalies[second], preferred_element_type=jnp.float32)
        covar = (weights_for(bin_value[None], points)[0] * cross / (MEMBERS - 1)).astype(jnp.bfloat16)
        to_first = jnp.dot(forcing[second], covar.T, preferred_element_type=jnp.float32)
        to_second = jnp.dot(forcing[first], covar, preferred_element_type=jnp.float32)
        total = total.at[first].add(to_first)
        total = total.at[second].add(to_second)
        return total, None

    slots = jnp.concatenate([pair_tiles.astype(jnp.int32), loc_bin.astype(jnp.int32)[:, None]], axis=1)
    increment, _ = lax.scan(pair_step, increment, slots)
    return (anomalies.astype(jnp.float32) + increment).astype(jnp.bfloat16)
```

```python
import functools

import jax
import jax.numpy as jnp
from jax import lax
from jax.experimental import pallas as pl
from jax.experimental.pallas import tpu as pltpu
from jax.sharding import PartitionSpec as P

MEMBERS = 256
POINTS = 512
NBIN = 4
RADIUS = 4
TILES = 4
SLOTS = 8
BLOCKS = 8
HALF = MEMBERS // 2
CHUNKS = 2
ROWS = HALF // CHUNKS
BAND = 128
MESH = pl.DeviceIdType.MESH


def kernel(
    obs_ref, pair_ref, bin_ref, a_ref, innov_ref, out_ref,
    before_pair, before_bin, a_win, a_turned, g_win0, g_win1, rho, cov, own_cov, to_first, to_second,
    i_left, i_right, from_left, from_right, own_total,
    a_send, a_recv, relay_send, relay_recv, g_send, g_recv, i_send, i_recv, info_send, info_recv,
):
    core = lax.axis_index("mem")
    me = lax.axis_index("tile")
    size = lax.axis_size("tile")
    right = (core, lax.rem(me + 1, size))
    left = (core, lax.rem(me + size - 1, size))
    sibling = (1 - core, me)
    g_win = (g_win0, g_win1)

    def send(src, dst, send_sem, recv_sem, device):
        return pltpu.make_async_remote_copy(
            src_ref=src, dst_ref=dst, send_sem=send_sem, recv_sem=recv_sem, device_id=device, device_id_type=MESH
        )

    barrier = pltpu.get_barrier_semaphore()
    for device in (left, right, sibling):
        pl.semaphore_signal(barrier, inc=1, device_id=device, device_id_type=MESH)
    pl.semaphore_wait(barrier, 3)

    mine = pl.ds(pl.multiple_of(core * HALF, HALF), HALF)
    a_out = []
    for t in range(TILES):
        for side, (device, slot) in enumerate(((right, t), (left, 2 * TILES + t), (sibling, TILES + t))):
            a_out.append(send(a_ref.at[t], a_win.at[slot, mine], a_send.at[side, t], a_recv.at[side, t], device))
            a_out[-1].start()
    info_out = [
        send(pair_ref, before_pair, info_send.at[0], info_recv.at[0], right),
        send(bin_ref, before_bin, info_send.at[1], info_recv.at[1], right),
    ]
    for copy in info_out:
        copy.start()

    base = me * TILES
    g_out = []
    for h in range(CHUNKS):
        for t in range(TILES):
            total = jnp.zeros((ROWS, POINTS), jnp.float32)
            for o in range(BLOCKS):
                share = jnp.where(obs_ref[o] - base == t, 1.0, 0.0).astype(jnp.float32)
                total = total + share * innov_ref[o, h * ROWS : (h + 1) * ROWS, :].astype(jnp.float32)
            g_win[h][TILES + t] = total.astype(jnp.bfloat16)
        here = g_win[h].at[TILES : 2 * TILES]
        for side, (device, slot) in enumerate(((right, 0), (left, 2 * TILES))):
            g_out.append(send(here, g_win[h].at[slot : slot + TILES], g_send.at[side, h], g_recv.at[side, h], device))
            g_out[-1].start()

    for t in range(TILES):
        a_win[TILES + t, mine] = a_ref[t]

    def weigh(n, _):
        b = n // (POINTS // BAND)
        start = pl.multiple_of(lax.rem(n, POINTS // BAND) * BAND, BAND)
        p = lax.broadcasted_iota(jnp.int32, (BAND, POINTS), 0) + start
        q = lax.broadcasted_iota(jnp.int32, (BAND, POINTS), 1)
        along = ((q & 31) - (p & 31)).astype(jnp.float32) + 0.5 * RADIUS * b.astype(jnp.float32)
        across = ((q >> 5) - (p >> 5)).astype(jnp.float32)
        weight = jnp.exp(-(along * along + across * across) / (2.0 * RADIUS * RADIUS))
        rho[b, pl.ds(start, BAND), :] = weight * (1.0 / (MEMBERS - 1))
        return 0

    lax.fori_loop(0, NBIN * (POINTS // BAND), weigh, 0)

    def product(turned, second, weights_of, target):
        for band in range(POINTS // BAND):
            rows = slice(band * BAND, (band + 1) * BAND)
            cross = jnp.dot(turned(rows), second, preferred_element_type=jnp.float32)
            target[rows, :] = (weights_of(rows) * cross).astype(jnp.bfloat16)

    for t in range(TILES):
        a_out[3 * t + 2].wait_recv()

    def own_product(t, _):
        tile = a_win[TILES + t]
        a_turned[TILES + t] = tile.T
        product(lambda rows: a_turned[TILES + t, rows, :], tile, lambda rows: rho[0, rows, :], own_cov.at[t])
        return 0

    lax.fori_loop(0, TILES, own_product, 0)

    relays = []
    for t in range(TILES):
        for side, slot in ((0, t), (1, 2 * TILES + t)):
            a_out[3 * t + side].wait_recv()
            here = a_win.at[slot, mine]
            relays.append(send(here, here, relay_send.at[side, t], relay_recv.at[side, t], sibling))
            relays[-1].start()
    for copy in info_out:
        copy.wait_recv()
    for copy in relays:
        copy.wait_recv()

    def turn(t, _):
        a_turned[t] = a_win[t].T
        return 0

    lax.fori_loop(0, TILES, turn, 0)

    base_before = lax.rem(me + size - 1, size) * TILES
    shift = base - TILES

    def slot_of(n):
        own = (pair_ref[n, 0] - shift, pair_ref[n, 1] - shift, bin_ref[n])
        far = (before_pair[n, 0] - base_before, before_pair[n, 1] - base_before, before_bin[n])
        return own, far

    def inside(first, second, b):
        return jnp.clip(first, 0, 2 * TILES - 1), jnp.clip(second, 0, 3 * TILES - 1), jnp.clip(b, 0, NBIN - 1)

    def covariance(n, _):
        for k, ends in enumerate(slot_of(n)):
            first, second, b = inside(*ends)
            product(
                lambda rows: a_turned[first, rows, :], a_win[second], lambda rows: rho[b, rows, :], cov.at[k * SLOTS + n]
            )
        return 0

    lax.fori_loop(0, SLOTS, covariance, 0)

    i_out = []
    nn = (((1,), (0,)), ((), ()))
    nt = (((1,), (1,)), ((), ()))
    for h in range(CHUNKS):
        g_out[2 * h].wait_recv()
        g_out[2 * h + 1].wait_recv()

        def increments(n, _):
            for k, ends in enumerate(slot_of(n)):
                first, second, _ = inside(*ends)
                matrix = cov[k * SLOTS + n]
                to_first[k * SLOTS + n] = lax.dot_general(
                    g_win[h][second], matrix, nt, preferred_element_type=jnp.float32
                )
                to_second[k * SLOTS + n] = lax.dot_general(
                    g_win[h][first], matrix, nn, preferred_element_type=jnp.float32
                )
            return 0

        lax.fori_loop(0, SLOTS, increments, 0)

        slots = [slot_of(n) for n in range(SLOTS)]

        def hit(end, tile, bin_, alive):
            return jnp.where((end == tile) & (bin_ < NBIN) & alive, 1.0, 0.0).astype(jnp.float32)

        near = [pair_ref[n, 1] - base < 2 * TILES for n in range(SLOTS)]
        away = [before_pair[n, 1] - base_before >= 2 * TILES for n in range(SLOTS)]
        for t in range(TILES):
            total = jnp.zeros((ROWS, POINTS), jnp.float32)
            for n, (_, (first, _, b)) in enumerate(slots):
                total = total + hit(first, t, b, away[n]) * to_first[SLOTS + n]
            i_left[h, t] = total.astype(jnp.bfloat16)
            total = jnp.zeros((ROWS, POINTS), jnp.float32)
            for n, ((_, second, b), (_, far_second, far_b)) in enumerate(slots):
                total = total + hit(second, 2 * TILES + t, b, near[n]) * to_second[n]
                total = total + hit(far_second, 2 * TILES + t, far_b, away[n]) * to_second[SLOTS + n]
            i_right[h, t] = total.astype(jnp.bfloat16)
        for side, (device, src, dst) in enumerate(((right, i_right, from_left), (left, i_left, from_right))):
            i_out.append(send(src.at[h], dst.at[h], i_send.at[side, h], i_recv.at[side, h], device))
            i_out[-1].start()
        for t in range(TILES):
            rows = slice(h * ROWS, (h + 1) * ROWS)
            total = jnp.dot(g_win[h][TILES + t], own_cov[t], preferred_element_type=jnp.float32)
            total = total + a_ref[t, rows, :].astype(jnp.float32)
            for n, ((first, second, b), _) in enumerate(slots):
                total = total + hit(first, TILES + t, b, near[n]) * to_first[n]
                total = total + hit(second, TILES + t, b, near[n]) * to_second[n]
            own_total[h, t] = total

    for h in range(CHUNKS):
        i_out[2 * h].wait_recv()
        i_out[2 * h + 1].wait_recv()
        for t in range(TILES):
            total = own_total[h, t] + from_left[h, t].astype(jnp.float32) + from_right[h, t].astype(jnp.float32)
            out_ref[t, h * ROWS : (h + 1) * ROWS, :] = total.astype(jnp.bfloat16)
    for copy in a_out + info_out + g_out + relays + i_out:
        copy.wait_send()


def per_device(anomalies, innovations, obs_tile, pair_tiles, loc_bin):
    bf16, f32 = jnp.bfloat16, jnp.float32
    vmem, smem = pl.BlockSpec(memory_space=pltpu.VMEM), pl.BlockSpec(memory_space=pltpu.SMEM)
    dma = pltpu.SemaphoreType.DMA
    return pl.pallas_call(
        kernel,
        name="analysis",
        out_shape=jax.ShapeDtypeStruct(anomalies.shape, bf16),
        in_specs=[smem, smem, smem, vmem, vmem],
        out_specs=vmem,
        scratch_shapes=[
            pltpu.SMEM((SLOTS, 2), jnp.int32),
            pltpu.SMEM((SLOTS,), jnp.int32),
            pltpu.VMEM((3 * TILES, MEMBERS, POINTS), bf16),
            pltpu.VMEM((2 * TILES, POINTS, MEMBERS), bf16),
            pltpu.VMEM((3 * TILES, ROWS, POINTS), bf16),
            pltpu.VMEM((3 * TILES, ROWS, POINTS), bf16),
            pltpu.VMEM((NBIN, POINTS, POINTS), f32),
            pltpu.VMEM((2 * SLOTS, POINTS, POINTS), bf16),
            pltpu.VMEM((TILES, POINTS, POINTS), bf16),
            pltpu.VMEM((2 * SLOTS, ROWS, POINTS), f32),
            pltpu.VMEM((2 * SLOTS, ROWS, POINTS), f32),
            pltpu.VMEM((CHUNKS, TILES, ROWS, POINTS), bf16),
            pltpu.VMEM((CHUNKS, TILES, ROWS, POINTS), bf16),
            pltpu.VMEM((CHUNKS, TILES, ROWS, POINTS), bf16),
            pltpu.VMEM((CHUNKS, TILES, ROWS, POINTS), bf16),
            pltpu.VMEM((CHUNKS, TILES, ROWS, POINTS), f32),
            dma((3, TILES)), dma((3, TILES)),
            dma((2, TILES)), dma((2, TILES)),
            dma((2, CHUNKS)), dma((2, CHUNKS)),
            dma((2, CHUNKS)), dma((2, CHUNKS)),
            dma((2,)), dma((2,)),
        ],
        compiler_params=pltpu.CompilerParams(collective_id=0, has_side_effects=True, vmem_limit_bytes=56 << 20),
    )(obs_tile, pair_tiles, loc_bin, anomalies, innovations)


def solution(mesh):
    return jax.shard_map(
        per_device,
        mesh=mesh,
        in_specs=(
            P("tile", "mem", None),
            P("tile", "mem", None),
            P("tile"),
            P("tile", None),
            P("tile"),
        ),
        out_specs=P("tile", "mem", None),
        check_vma=False,
    )
```

```python
import functools

import jax
import jax.numpy as jnp
from jax import lax
from jax.experimental import pallas as pl
from jax.experimental.pallas import tpu as pltpu
from jax.sharding import PartitionSpec as P

MEMBERS = 256
POINTS = 512
NBIN = 4
RADIUS = 4
TILES = 4
SLOTS = 8
BLOCKS = 8
HALF = MEMBERS // 2
CHUNKS = 2
ROWS = HALF // CHUNKS
BAND = 128
MESH = pl.DeviceIdType.MESH


def kernel(
    obs_ref, pair_ref, bin_ref, a_ref, innov_ref, out_ref,
    before_pair, before_bin, a_win, a_turned, g_win0, g_win1, rho, cov, own_cov, to_first, to_second,
    i_left, i_right, from_left, from_right, own_total,
    a_send, a_recv, relay_send, relay_recv, g_send, g_recv, i_send, i_recv, info_send, info_recv,
):
    core = lax.axis_index("mem")
    me = lax.axis_index("tile")
    size = lax.axis_size("tile")
    right = (core, lax.rem(me + 1, size))
    left = (core, lax.rem(me + size - 1, size))
    sibling = (1 - core, me)
    g_win = (g_win0, g_win1)

    def send(src, dst, send_sem, recv_sem, device):
        return pltpu.make_async_remote_copy(
            src_ref=src, dst_ref=dst, send_sem=send_sem, recv_sem=recv_sem, device_id=device, device_id_type=MESH
        )

    not_first, not_last = me > 0, me < size - 1
    to_side, from_side = (not_last, not_first), (not_first, not_last)

    barrier = pltpu.get_barrier_semaphore()
    for device, there in ((left, not_first), (right, not_last), (sibling, None)):

        def greet():
            pl.semaphore_signal(barrier, inc=1, device_id=device, device_id_type=MESH)

        greet() if there is None else pl.when(there)(greet)
    both = not_first & not_last

    @pl.when(both)
    def _():
        pl.semaphore_wait(barrier, 3)

    @pl.when(jnp.logical_not(both))
    def _():
        pl.semaphore_wait(barrier, 2)

    mine = pl.ds(pl.multiple_of(core * HALF, HALF), HALF)
    a_out = [[], [], []]
    for t in range(TILES):
        for side, (device, slot) in enumerate(((right, t), (left, 2 * TILES + t), (sibling, TILES + t))):
            a_out[side].append(send(a_ref.at[t], a_win.at[slot, mine], a_send.at[side, t], a_recv.at[side, t], device))
    info_out = [
        send(pair_ref, before_pair, info_send.at[0], info_recv.at[0], right),
        send(bin_ref, before_bin, info_send.at[1], info_recv.at[1], right),
    ]
    for t in range(TILES):
        for side in range(2):
            pl.when(to_side[side])(a_out[side][t].start)
        a_out[2][t].start()

    @pl.when(not_last)
    def _():
        for copy in info_out:
            copy.start()

    @pl.when(me == 0)
    def _():
        a_win[:TILES] = jnp.zeros((TILES, MEMBERS, POINTS), jnp.bfloat16)
        for h in range(CHUNKS):
            g_win[h][:TILES] = jnp.zeros((TILES, ROWS, POINTS), jnp.bfloat16)
        from_left[...] = jnp.zeros_like(from_left)
        for n in range(SLOTS):
            before_bin[n] = NBIN
            before_pair[n, 0] = 0
            before_pair[n, 1] = 0

    @pl.when(me == size - 1)
    def _():
        a_win[2 * TILES :] = jnp.zeros((TILES, MEMBERS, POINTS), jnp.bfloat16)
        for h in range(CHUNKS):
            g_win[h][2 * TILES :] = jnp.zeros((TILES, ROWS, POINTS), jnp.bfloat16)
        from_right[...] = jnp.zeros_like(from_right)

    base = me * TILES
    g_out = [[], []]
    for h in range(CHUNKS):
        for t in range(TILES):
            total = jnp.zeros((ROWS, POINTS), jnp.float32)
            for o in range(BLOCKS):
                share = jnp.where(obs_ref[o] - base == t, 1.0, 0.0).astype(jnp.float32)
                total = total + share * innov_ref[o, h * ROWS : (h + 1) * ROWS, :].astype(jnp.float32)
            g_win[h][TILES + t] = total.astype(jnp.bfloat16)
        here = g_win[h].at[TILES : 2 * TILES]
        for side, (device, slot) in enumerate(((right, 0), (left, 2 * TILES))):
            there = g_win[h].at[slot : slot + TILES]
            g_out[side].append(send(here, there, g_send.at[side, h], g_recv.at[side, h], device))
            pl.when(to_side[side])(g_out[side][h].start)

    for t in range(TILES):
        a_win[TILES + t, mine] = a_ref[t]

    def weigh(n, _):
        b = n // (POINTS // BAND)
        start = pl.multiple_of(lax.rem(n, POINTS // BAND) * BAND, BAND)
        p = lax.broadcasted_iota(jnp.int32, (BAND, POINTS), 0) + start
        q = lax.broadcasted_iota(jnp.int32, (BAND, POINTS), 1)
        along = ((q & 31) - (p & 31)).astype(jnp.float32) + 0.5 * RADIUS * b.astype(jnp.float32)
        across = ((q >> 5) - (p >> 5)).astype(jnp.float32)
        weight = jnp.exp(-(along * along + across * across) / (2.0 * RADIUS * RADIUS))
        rho[b, pl.ds(start, BAND), :] = weight * (1.0 / (MEMBERS - 1))
        return 0

    lax.fori_loop(0, NBIN * (POINTS // BAND), weigh, 0)

    def product(turned, second, weights_of, target):
        for band in range(POINTS // BAND):
            rows = slice(band * BAND, (band + 1) * BAND)
            cross = jnp.dot(turned(rows), second, preferred_element_type=jnp.float32)
            target[rows, :] = (weights_of(rows) * cross).astype(jnp.bfloat16)

    for t in range(TILES):
        a_out[2][t].wait_recv()

    def own_product(t, _):
        tile = a_win[TILES + t]
        a_turned[TILES + t] = tile.T
        product(lambda rows: a_turned[TILES + t, rows, :], tile, lambda rows: rho[0, rows, :], own_cov.at[t])
        return 0

    lax.fori_loop(0, TILES, own_product, 0)

    relays = [[], []]
    for t in range(TILES):
        for side, slot in ((0, t), (1, 2 * TILES + t)):
            here = a_win.at[slot, mine]
            relays[side].append(send(here, here, relay_send.at[side, t], relay_recv.at[side, t], sibling))

            @pl.when(from_side[side])
            def _():
                a_out[side][t].wait_recv()
                relays[side][t].start()

    @pl.when(not_first)
    def _():
        for copy in info_out + relays[0]:
            copy.wait_recv()

    @pl.when(not_last)
    def _():
        for copy in relays[1]:
            copy.wait_recv()

    def turn(t, _):
        a_turned[t] = a_win[t].T
        return 0

    lax.fori_loop(0, TILES, turn, 0)

    base_before = lax.rem(me + size - 1, size) * TILES
    shift = base - TILES

    def slot_of(n):
        own = (pair_ref[n, 0] - shift, pair_ref[n, 1] - shift, bin_ref[n])
        far = (before_pair[n, 0] - base_before, before_pair[n, 1] - base_before, before_bin[n])
        return own, far

    def inside(first, second, b):
        return jnp.clip(first, 0, 2 * TILES - 1), jnp.clip(second, 0, 3 * TILES - 1), jnp.clip(b, 0, NBIN - 1)

    def covariance(n, _):
        for k, ends in enumerate(slot_of(n)):
            first, second, b = inside(*ends)
            product(
                lambda rows: a_turned[first, rows, :], a_win[second], lambda rows: rho[b, rows, :], cov.at[k * SLOTS + n]
            )
        return 0

    lax.fori_loop(0, SLOTS, covariance, 0)

    i_out = [[], []]
    nn = (((1,), (0,)), ((), ()))
    nt = (((1,), (1,)), ((), ()))
    for h in range(CHUNKS):
        for side in range(2):
            pl.when(from_side[side])(g_out[side][h].wait_recv)

        def increments(n, _):
            for k, ends in enumerate(slot_of(n)):
                first, second, _ = inside(*ends)
                matrix = cov[k * SLOTS + n]
                to_first[k * SLOTS + n] = lax.dot_general(
                    g_win[h][second], matrix, nt, preferred_element_type=jnp.float32
                )
                to_second[k * SLOTS + n] = lax.dot_general(
                    g_win[h][first], matrix, nn, preferred_element_type=jnp.float32
                )
            return 0

        lax.fori_loop(0, SLOTS, increments, 0)

        slots = [slot_of(n) for n in range(SLOTS)]

        def hit(end, tile, bin_, alive):
            return jnp.where((end == tile) & (bin_ < NBIN) & alive, 1.0, 0.0).astype(jnp.float32)

        near = [pair_ref[n, 1] - base < 2 * TILES for n in range(SLOTS)]
        away = [before_pair[n, 1] - base_before >= 2 * TILES for n in range(SLOTS)]
        for t in range(TILES):
            total = jnp.zeros((ROWS, POINTS), jnp.float32)
            for n, (_, (first, _, b)) in enumerate(slots):
                total = total + hit(first, t, b, away[n]) * to_first[SLOTS + n]
            i_left[h, t] = total.astype(jnp.bfloat16)
            total = jnp.zeros((ROWS, POINTS), jnp.float32)
            for n, ((_, second, b), (_, far_second, far_b)) in enumerate(slots):
                total = total + hit(second, 2 * TILES + t, b, near[n]) * to_second[n]
                total = total + hit(far_second, 2 * TILES + t, far_b, away[n]) * to_second[SLOTS + n]
            i_right[h, t] = total.astype(jnp.bfloat16)
        for side, (device, src, dst) in enumerate(((right, i_right, from_left), (left, i_left, from_right))):
            i_out[side].append(send(src.at[h], dst.at[h], i_send.at[side, h], i_recv.at[side, h], device))
            pl.when(to_side[side])(i_out[side][h].start)
        for t in range(TILES):
            rows = slice(h * ROWS, (h + 1) * ROWS)
            total = jnp.dot(g_win[h][TILES + t], own_cov[t], preferred_element_type=jnp.float32)
            total = total + a_ref[t, rows, :].astype(jnp.float32)
            for n, ((first, second, b), _) in enumerate(slots):
                total = total + hit(first, TILES + t, b, near[n]) * to_first[n]
                total = total + hit(second, TILES + t, b, near[n]) * to_second[n]
            own_total[h, t] = total

    for h in range(CHUNKS):
        for side in range(2):
            pl.when(from_side[side])(i_out[side][h].wait_recv)
        for t in range(TILES):
            total = own_total[h, t] + from_left[h, t].astype(jnp.float32) + from_right[h, t].astype(jnp.float32)
            out_ref[t, h * ROWS : (h + 1) * ROWS, :] = total.astype(jnp.bfloat16)

    for copy in a_out[2]:
        copy.wait_send()
    for side in range(2):

        @pl.when(to_side[side])
        def _():
            for copy in a_out[side] + g_out[side] + i_out[side]:
                copy.wait_send()

        @pl.when(from_side[side])
        def _():
            for copy in relays[side]:
                copy.wait_send()

    @pl.when(not_last)
    def _():
        for copy in info_out:
            copy.wait_send()


def per_device(anomalies, innovations, obs_tile, pair_tiles, loc_bin):
    bf16, f32 = jnp.bfloat16, jnp.float32
    vmem, smem = pl.BlockSpec(memory_space=pltpu.VMEM), pl.BlockSpec(memory_space=pltpu.SMEM)
    dma = pltpu.SemaphoreType.DMA
    return pl.pallas_call(
        kernel,
        name="analysis",
        out_shape=jax.ShapeDtypeStruct(anomalies.shape, bf16),
        in_specs=[smem, smem, smem, vmem, vmem],
        out_specs=vmem,
        scratch_shapes=[
            pltpu.SMEM((SLOTS, 2), jnp.int32),
            pltpu.SMEM((SLOTS,), jnp.int32),
            pltpu.VMEM((3 * TILES, MEMBERS, POINTS), bf16),
            pltpu.VMEM((2 * TILES, POINTS, MEMBERS), bf16),
            pltpu.VMEM((3 * TILES, ROWS, POINTS), bf16),
            pltpu.VMEM((3 * TILES, ROWS, POINTS), bf16),
            pltpu.VMEM((NBIN, POINTS, POINTS), f32),
            pltpu.VMEM((2 * SLOTS, POINTS, POINTS), bf16),
            pltpu.VMEM((TILES, POINTS, POINTS), bf16),
            pltpu.VMEM((2 * SLOTS, ROWS, POINTS), f32),
            pltpu.VMEM((2 * SLOTS, ROWS, POINTS), f32),
            pltpu.VMEM((CHUNKS, TILES, ROWS, POINTS), bf16),
            pltpu.VMEM((CHUNKS, TILES, ROWS, POINTS), bf16),
            pltpu.VMEM((CHUNKS, TILES, ROWS, POINTS), bf16),
            pltpu.VMEM((CHUNKS, TILES, ROWS, POINTS), bf16),
            pltpu.VMEM((CHUNKS, TILES, ROWS, POINTS), f32),
            dma((3, TILES)), dma((3, TILES)),
            dma((2, TILES)), dma((2, TILES)),
            dma((2, CHUNKS)), dma((2, CHUNKS)),
            dma((2, CHUNKS)), dma((2, CHUNKS)),
            dma((2,)), dma((2,)),
        ],
        compiler_params=pltpu.CompilerParams(collective_id=0, has_side_effects=True, vmem_limit_bytes=56 << 20),
    )(obs_tile, pair_tiles, loc_bin, anomalies, innovations)


def solution(mesh):
    return jax.shard_map(
        per_device,
        mesh=mesh,
        in_specs=(
            P("tile", "mem", None),
            P("tile", "mem", None),
            P("tile"),
            P("tile", None),
            P("tile"),
        ),
        out_specs=P("tile", "mem", None),
        check_vma=False,
    )
```

```python
import functools

import jax
import jax.numpy as jnp
from jax import lax
from jax.experimental import pallas as pl
from jax.experimental.pallas import tpu as pltpu
from jax.sharding import PartitionSpec as P

MEMBERS = 256
POINTS = 512
NBIN = 4
RADIUS = 4
TILES = 4
SLOTS = 8
BLOCKS = 8
HALF = MEMBERS // 2
CHUNKS = 2
ROWS = HALF // CHUNKS
BAND = 128
MESH = pl.DeviceIdType.MESH


def kernel(
    obs_ref, pair_ref, bin_ref, a_ref, innov_hbm, out_ref,
    innov_ref, before_pair, before_bin, a_win, a_turned, g_win0, g_win1, rho, cov, cov_turned, own_cov, to_first, to_second,
    i_left, i_right, from_left, from_right, own_total,
    a_send, a_recv, relay_send, relay_recv, g_send, g_recv, i_send, i_recv, info_send, info_recv, load_sem,
):
    core = lax.axis_index("mem")
    me = lax.axis_index("tile")
    size = lax.axis_size("tile")
    right = (core, lax.rem(me + 1, size))
    left = (core, lax.rem(me + size - 1, size))
    sibling = (1 - core, me)
    g_win = (g_win0, g_win1)

    def send(src, dst, send_sem, recv_sem, device):
        return pltpu.make_async_remote_copy(
            src_ref=src, dst_ref=dst, send_sem=send_sem, recv_sem=recv_sem, device_id=device, device_id_type=MESH
        )

    mine = pl.ds(pl.multiple_of(core * HALF, HALF), HALF)
    load_innov = pltpu.make_async_copy(innov_hbm, innov_ref, load_sem.at[0])
    load_a = pltpu.make_async_copy(a_ref, a_win.at[TILES : 2 * TILES, mine], load_sem.at[1])
    load_innov.start()
    load_a.start()

    not_first, not_last = me > 0, me < size - 1
    to_side, from_side = (not_last, not_first), (not_first, not_last)

    barrier = pltpu.get_barrier_semaphore()
    for device, there in ((left, not_first), (right, not_last), (sibling, None)):

        def greet():
            pl.semaphore_signal(barrier, inc=1, device_id=device, device_id_type=MESH)

        greet() if there is None else pl.when(there)(greet)
    both = not_first & not_last

    @pl.when(both)
    def _():
        pl.semaphore_wait(barrier, 3)

    @pl.when(jnp.logical_not(both))
    def _():
        pl.semaphore_wait(barrier, 2)

    a_out = [[], [], []]
    for t in range(TILES):
        for side, (device, slot) in enumerate(((right, t), (left, 2 * TILES + t), (sibling, TILES + t))):
            a_out[side].append(send(a_ref.at[t], a_win.at[slot, mine], a_send.at[side, t], a_recv.at[side, t], device))
    info_out = [
        send(pair_ref, before_pair, info_send.at[0], info_recv.at[0], right),
        send(bin_ref, before_bin, info_send.at[1], info_recv.at[1], right),
    ]
    for t in range(TILES):
        for side in range(2):
            pl.when(to_side[side])(a_out[side][t].start)
        a_out[2][t].start()

    @pl.when(not_last)
    def _():
        for copy in info_out:
            copy.start()

    @pl.when(me == 0)
    def _():
        a_win[:TILES] = jnp.zeros((TILES, MEMBERS, POINTS), jnp.bfloat16)
        for h in range(CHUNKS):
            g_win[h][:TILES] = jnp.zeros((TILES, ROWS, POINTS), jnp.bfloat16)
        from_left[...] = jnp.zeros_like(from_left)
        for n in range(SLOTS):
            before_bin[n] = NBIN
            before_pair[0, n] = 0
            before_pair[1, n] = 0

    @pl.when(me == size - 1)
    def _():
        a_win[2 * TILES :] = jnp.zeros((TILES, MEMBERS, POINTS), jnp.bfloat16)
        for h in range(CHUNKS):
            g_win[h][2 * TILES :] = jnp.zeros((TILES, ROWS, POINTS), jnp.bfloat16)
        from_right[...] = jnp.zeros_like(from_right)

    load_innov.wait()
    base = me * TILES
    g_out = [[], []]
    for h in range(CHUNKS):
        for t in range(TILES):
            total = jnp.zeros((ROWS, POINTS), jnp.float32)
            for o in range(BLOCKS):
                share = jnp.where(obs_ref[o] - base == t, 1.0, 0.0).astype(jnp.float32)
                total = total + share * innov_ref[o, h * ROWS : (h + 1) * ROWS, :].astype(jnp.float32)
            g_win[h][TILES + t] = total.astype(jnp.bfloat16)
        here = g_win[h].at[TILES : 2 * TILES]
        for side, (device, slot) in enumerate(((right, 0), (left, 2 * TILES))):
            there = g_win[h].at[slot : slot + TILES]
            g_out[side].append(send(here, there, g_send.at[side, h], g_recv.at[side, h], device))

    def weigh(n, _):
        b = n // (POINTS // BAND)
        start = pl.multiple_of(lax.rem(n, POINTS // BAND) * BAND, BAND)
        p = lax.broadcasted_iota(jnp.int32, (BAND, POINTS), 0) + start
        q = lax.broadcasted_iota(jnp.int32, (BAND, POINTS), 1)
        along = ((q & 31) - (p & 31)).astype(jnp.float32) + 0.5 * RADIUS * b.astype(jnp.float32)
        across = ((q >> 5) - (p >> 5)).astype(jnp.float32)
        weight = jnp.exp(-(along * along + across * across) / (2.0 * RADIUS * RADIUS))
        rho[b, pl.ds(start, BAND), :] = weight * (1.0 / (MEMBERS - 1))
        return 0

    lax.fori_loop(0, NBIN * (POINTS // BAND), weigh, 0)

    def product(turned, second, weights_of, target, also_turned=None):
        for band in range(POINTS // BAND):
            rows = slice(band * BAND, (band + 1) * BAND)
            cross = jnp.dot(turned(rows), second, preferred_element_type=jnp.float32)
            rounded = (weights_of(rows) * cross).astype(jnp.bfloat16)
            target[rows, :] = rounded
            if also_turned is not None:
                also_turned[:, rows] = rounded.T

    load_a.wait()
    for t in range(TILES):
        a_out[2][t].wait_recv()

    def own_product(t, _):
        tile = a_win[TILES + t]
        a_turned[TILES + t] = tile.T
        product(lambda rows: a_turned[TILES + t, rows, :], tile, lambda rows: rho[0, rows, :], own_cov.at[t])
        return 0

    lax.fori_loop(0, TILES, own_product, 0)

    relays = [[], []]
    for t in range(TILES):
        for side, slot in ((0, t), (1, 2 * TILES + t)):
            here = a_win.at[slot, mine]
            relays[side].append(send(here, here, relay_send.at[side, t], relay_recv.at[side, t], sibling))

            @pl.when(from_side[side])
            def _():
                a_out[side][t].wait_recv()
                relays[side][t].start()

        for h, when in enumerate((2, 3)):
            if when == t:
                for side in range(2):
                    pl.when(to_side[side])(g_out[side][h].start)

    @pl.when(not_first)
    def _():
        for copy in info_out + relays[0]:
            copy.wait_recv()

    @pl.when(not_last)
    def _():
        for copy in relays[1]:
            copy.wait_recv()

    def turn(t, _):
        a_turned[t] = a_win[t].T
        return 0

    lax.fori_loop(0, TILES, turn, 0)

    base_before = lax.rem(me + size - 1, size) * TILES
    shift = base - TILES

    def slot_of(n):
        own = (pair_ref[0, n] - shift, pair_ref[1, n] - shift, bin_ref[n])
        far = (before_pair[0, n] - base_before, before_pair[1, n] - base_before, before_bin[n])
        return own, far

    def inside(first, second, b):
        return jnp.clip(first, 0, 2 * TILES - 1), jnp.clip(second, 0, 3 * TILES - 1), jnp.clip(b, 0, NBIN - 1)

    def covariance(n, _):
        for k, ends in enumerate(slot_of(n)):
            first, second, b = inside(*ends)
            product(
                lambda rows: a_turned[first, rows, :], a_win[second], lambda rows: rho[b, rows, :], cov.at[k * SLOTS + n],
                cov_turned.at[k * SLOTS + n],
            )
        return 0

    lax.fori_loop(0, SLOTS, covariance, 0)

    i_out = [[], []]
    slots = [slot_of(n) for n in range(SLOTS)]

    def hit(end, tile, bin_, alive):
        return jnp.where((end == tile) & (bin_ < NBIN) & alive, 1.0, 0.0).astype(jnp.float32)

    near = [pair_ref[1, n] - base < 2 * TILES for n in range(SLOTS)]
    away = [before_pair[1, n] - base_before >= 2 * TILES for n in range(SLOTS)]
    for h in range(CHUNKS):
        for side in range(2):
            pl.when(from_side[side])(g_out[side][h].wait_recv)

        def increments(n, _):
            for k, ends in enumerate(slot_of(n)):
                first, second, _ = inside(*ends)
                u = k * SLOTS + n
                to_first[h, u] = jnp.dot(g_win[h][second], cov_turned[u], preferred_element_type=jnp.float32)
                to_second[h, u] = jnp.dot(g_win[h][first], cov[u], preferred_element_type=jnp.float32)
            return 0

        lax.fori_loop(0, SLOTS, increments, 0)

        for t in range(TILES):
            total = jnp.zeros((ROWS, POINTS), jnp.float32)
            for n, (_, (first, _, b)) in enumerate(slots):
                total = total + hit(first, t, b, away[n]) * to_first[h, SLOTS + n]
            i_left[h, t] = total.astype(jnp.bfloat16)
            total = jnp.zeros((ROWS, POINTS), jnp.float32)
            for n, ((_, second, b), (_, far_second, far_b)) in enumerate(slots):
                total = total + hit(second, 2 * TILES + t, b, near[n]) * to_second[h, n]
                total = total + hit(far_second, 2 * TILES + t, far_b, away[n]) * to_second[h, SLOTS + n]
            i_right[h, t] = total.astype(jnp.bfloat16)
        for side, (device, src, dst) in enumerate(((right, i_right, from_left), (left, i_left, from_right))):
            i_out[side].append(send(src.at[h], dst.at[h], i_send.at[side, h], i_recv.at[side, h], device))
            pl.when(to_side[side])(i_out[side][h].start)

    for h in range(CHUNKS):
        rows = pl.ds(pl.multiple_of(core * HALF + h * ROWS, ROWS), ROWS)
        for t in range(TILES):
            total = jnp.dot(g_win[h][TILES + t], own_cov[t], preferred_element_type=jnp.float32)
            total = total + a_win[TILES + t, rows, :].astype(jnp.float32)
            for n, ((first, second, b), _) in enumerate(slots):
                total = total + hit(first, TILES + t, b, near[n]) * to_first[h, n]
                total = total + hit(second, TILES + t, b, near[n]) * to_second[h, n]
            own_total[h, t] = total

    for h in range(CHUNKS):
        for side in range(2):
            pl.when(from_side[side])(i_out[side][h].wait_recv)
        for t in range(TILES):
            total = own_total[h, t] + from_left[h, t].astype(jnp.float32) + from_right[h, t].astype(jnp.float32)
            out_ref[t, h * ROWS : (h + 1) * ROWS, :] = total.astype(jnp.bfloat16)

    for copy in a_out[2]:
        copy.wait_send()
    for side in range(2):

        @pl.when(to_side[side])
        def _():
            for copy in a_out[side] + g_out[side] + i_out[side]:
                copy.wait_send()

        @pl.when(from_side[side])
        def _():
            for copy in relays[side]:
                copy.wait_send()

    @pl.when(not_last)
    def _():
        for copy in info_out:
            copy.wait_send()


def hand_on(src, dst, sem):
    copy = pltpu.make_async_copy(src, dst, sem)
    copy.start()
    copy.wait()


def per_device(anomalies, innovations, obs_tile, pair_tiles, loc_bin):
    bf16, f32 = jnp.bfloat16, jnp.float32
    vmem, smem = pl.BlockSpec(memory_space=pltpu.VMEM), pl.BlockSpec(memory_space=pltpu.SMEM)
    hbm = pl.BlockSpec(memory_space=pl.ANY)
    dma = pltpu.SemaphoreType.DMA
    made = pl.pallas_call(
        kernel,
        name="analysis",
        out_shape=pltpu.VMEM(anomalies.shape, bf16),
        in_specs=[smem, smem, smem, hbm, hbm],
        out_specs=vmem,
        scratch_shapes=[
            pltpu.VMEM(innovations.shape, bf16),
            pltpu.SMEM((2, SLOTS), jnp.int32),
            pltpu.SMEM((SLOTS,), jnp.int32),
            pltpu.VMEM((3 * TILES, MEMBERS, POINTS), bf16),
            pltpu.VMEM((2 * TILES, POINTS, MEMBERS), bf16),
            pltpu.VMEM((3 * TILES, ROWS, POINTS), bf16),
            pltpu.VMEM((3 * TILES, ROWS, POINTS), bf16),
            pltpu.VMEM((NBIN, POINTS, POINTS), f32),
            pltpu.VMEM((2 * SLOTS, POINTS, POINTS), bf16),
            pltpu.VMEM((2 * SLOTS, POINTS, POINTS), bf16),
            pltpu.VMEM((TILES, POINTS, POINTS), bf16),
            pltpu.VMEM((CHUNKS, 2 * SLOTS, ROWS, POINTS), f32),
            pltpu.VMEM((CHUNKS, 2 * SLOTS, ROWS, POINTS), f32),
            pltpu.VMEM((CHUNKS, TILES, ROWS, POINTS), bf16),
            pltpu.VMEM((CHUNKS, TILES, ROWS, POINTS), bf16),
            pltpu.VMEM((CHUNKS, TILES, ROWS, POINTS), bf16),
            pltpu.VMEM((CHUNKS, TILES, ROWS, POINTS), bf16),
            pltpu.VMEM((CHUNKS, TILES, ROWS, POINTS), f32),
            dma((3, TILES)), dma((3, TILES)),
            dma((2, TILES)), dma((2, TILES)),
            dma((2, CHUNKS)), dma((2, CHUNKS)),
            dma((2, CHUNKS)), dma((2, CHUNKS)),
            dma((2,)), dma((2,)), dma((2,)),
        ],
        compiler_params=pltpu.CompilerParams(collective_id=0, has_side_effects=True, vmem_limit_bytes=56 << 20),
    )(obs_tile, pair_tiles.T, loc_bin, anomalies, innovations)
    return pl.pallas_call(
        hand_on,
        name="hand_on",
        out_shape=jax.ShapeDtypeStruct(anomalies.shape, bf16),
        in_specs=[vmem],
        out_specs=hbm,
        scratch_shapes=[pltpu.SemaphoreType.DMA],
    )(pltpu.with_memory_space_constraint(made, pltpu.VMEM))


def solution(mesh):
    return jax.shard_map(
        per_device,
        mesh=mesh,
        in_specs=(
            P("tile", "mem", None),
            P("tile", "mem", None),
            P("tile"),
            P("tile", None),
            P("tile"),
        ),
        out_specs=P("tile", "mem", None),
        check_vma=False,
    )
```

```python
import functools

import jax
import jax.numpy as jnp
from jax import lax
from jax.experimental import pallas as pl
from jax.experimental.pallas import tpu as pltpu
from jax.sharding import PartitionSpec as P

MEMBERS = 256
POINTS = 512
NBIN = 4
RADIUS = 4
TILES = 4
SLOTS = 8
BLOCKS = 8
HALF = MEMBERS // 2
CHUNKS = 2
ROWS = HALF // CHUNKS
BAND = 128
UNROLL = 2
TALL = 256
MESH = pl.DeviceIdType.MESH


def kernel(
    obs_ref, pair_ref, bin_ref, a_ref, innov_hbm, out_ref,
    innov_ref, before_pair, before_bin, a_left, a_near, a_turned, g_own, g_left0, g_left1, g_near0, g_near1,
    rho, cov, cov_turned, own_cov, near_second, far_first, far_second,
    right_sum, own_sum, i_left, i_right, from_left, from_right,
    a_send, a_recv, relay_send, relay_recv, g_send, g_recv, i_send, i_recv, info_send, info_recv, load_sem,
):
    core = lax.axis_index("mem")
    me = lax.axis_index("tile")
    size = lax.axis_size("tile")
    right = (core, lax.rem(me + 1, size))
    left = (core, lax.rem(me + size - 1, size))
    sibling = (1 - core, me)
    g_left, g_near = (g_left0, g_left1), (g_near0, g_near1)

    def send(src, dst, send_sem, recv_sem, device):
        return pltpu.make_async_remote_copy(
            src_ref=src, dst_ref=dst, send_sem=send_sem, recv_sem=recv_sem, device_id=device, device_id_type=MESH
        )

    mine = pl.ds(pl.multiple_of(core * HALF, HALF), HALF)
    load_innov = pltpu.make_async_copy(innov_hbm, innov_ref, load_sem.at[0])
    load_a = pltpu.make_async_copy(a_ref, a_near.at[:TILES, mine], load_sem.at[1])
    load_innov.start()
    load_a.start()

    not_first, not_last = me > 0, me < size - 1
    to_side, from_side = (not_last, not_first), (not_first, not_last)

    barrier = pltpu.get_barrier_semaphore()
    for device, there in ((left, not_first), (right, not_last), (sibling, None)):

        def greet():
            pl.semaphore_signal(barrier, inc=1, device_id=device, device_id_type=MESH)

        greet() if there is None else pl.when(there)(greet)
    both = not_first & not_last

    @pl.when(both)
    def _():
        pl.semaphore_wait(barrier, 3)

    @pl.when(jnp.logical_not(both))
    def _():
        pl.semaphore_wait(barrier, 2)

    a_out = [[], [], []]
    for t in range(TILES):
        for side, (device, there) in enumerate(
            ((right, a_left.at[t, mine]), (left, a_near.at[TILES + t, mine]), (sibling, a_near.at[t, mine]))
        ):
            a_out[side].append(send(a_ref.at[t], there, a_send.at[side, t], a_recv.at[side, t], device))
    info_out = [
        send(pair_ref, before_pair, info_send.at[0], info_recv.at[0], right),
        send(bin_ref, before_bin, info_send.at[1], info_recv.at[1], right),
    ]
    for t in range(TILES):
        for side in range(2):
            pl.when(to_side[side])(a_out[side][t].start)
        a_out[2][t].start()

    @pl.when(not_last)
    def _():
        for copy in info_out:
            copy.start()

    @pl.when(me == 0)
    def _():
        a_left[...] = jnp.zeros_like(a_left)
        from_left[...] = jnp.zeros_like(from_left)
        for h in range(CHUNKS):
            g_left[h][...] = jnp.zeros_like(g_left[h])
        for n in range(SLOTS):
            before_bin[n] = NBIN
            before_pair[0, n] = 0
            before_pair[1, n] = 0

    @pl.when(me == size - 1)
    def _():
        a_near[TILES:] = jnp.zeros((TILES, MEMBERS, POINTS), jnp.bfloat16)
        from_right[...] = jnp.zeros_like(from_right)
        for h in range(CHUNKS):
            g_near[h][TILES:] = jnp.zeros((TILES, ROWS, POINTS), jnp.bfloat16)

    load_innov.wait()
    base = me * TILES
    g_out = [[], []]
    for h in range(CHUNKS):
        rows = slice(h * ROWS, (h + 1) * ROWS)
        for t in range(TILES):
            total = jnp.zeros((ROWS, POINTS), jnp.float32)
            for o in range(BLOCKS):
                share = jnp.where(obs_ref[o] - base == t, 1.0, 0.0).astype(jnp.float32)
                total = total + share * innov_ref[o, rows, :].astype(jnp.float32)
            g_own[t, rows, :] = total.astype(jnp.bfloat16)
            g_near[h][t] = total.astype(jnp.bfloat16)
        here = g_own.at[:, rows]
        for side, (device, there) in enumerate(((right, g_left[h]), (left, g_near[h].at[TILES:]))):
            g_out[side].append(send(here, there, g_send.at[side, h], g_recv.at[side, h], device))

    def weigh(n, _):
        b = n // (POINTS // BAND)
        start = pl.multiple_of(lax.rem(n, POINTS // BAND) * BAND, BAND)
        p = lax.broadcasted_iota(jnp.int32, (BAND, POINTS), 0) + start
        q = lax.broadcasted_iota(jnp.int32, (BAND, POINTS), 1)
        along = ((q & 31) - (p & 31)).astype(jnp.float32) + 0.5 * RADIUS * b.astype(jnp.float32)
        across = ((q >> 5) - (p >> 5)).astype(jnp.float32)
        weight = jnp.exp(-(along * along + across * across) / (2.0 * RADIUS * RADIUS))
        rho[b, pl.ds(start, BAND), :] = weight * (1.0 / (MEMBERS - 1))
        return 0

    lax.fori_loop(0, NBIN * (POINTS // BAND), weigh, 0)

    def product(turned, second, weights_of, target, also_turned=None):
        for band in range(POINTS // TALL):
            rows = slice(band * TALL, (band + 1) * TALL)
            cross = jnp.dot(turned(rows), second, preferred_element_type=jnp.float32)
            rounded = (weights_of(rows) * cross).astype(jnp.bfloat16)
            target[rows, :] = rounded
            if also_turned is not None:
                also_turned[:, rows] = rounded.T

    load_a.wait()
    for t in range(TILES):
        a_out[2][t].wait_recv()

    def own_product(t, _):
        tile = a_near[t]
        a_turned[TILES + t] = tile.T
        product(lambda rows: a_turned[TILES + t, rows, :], tile, lambda rows: rho[0, rows, :], own_cov.at[t])
        return 0

    lax.fori_loop(0, TILES, own_product, 0)

    relays = [[], []]
    for t in range(TILES):
        for side, here in ((0, a_left.at[t, mine]), (1, a_near.at[TILES + t, mine])):
            relays[side].append(send(here, here, relay_send.at[side, t], relay_recv.at[side, t], sibling))

            @pl.when(from_side[side])
            def _():
                a_out[side][t].wait_recv()
                relays[side][t].start()

        if t == TILES - 2:
            for side in range(2):
                pl.when(to_side[side])(g_out[side][0].start)


    @pl.when(not_last)
    def _():
        for copy in relays[1]:
            copy.wait_recv()

    for side in range(2):
        pl.when(to_side[side])(g_out[side][1].start)

    near = [(pair_ref[0, n] - base, pair_ref[1, n] - base, bin_ref[n]) for n in range(SLOTS)]

    def near_covariance(n, _):
        first = jnp.clip(pair_ref[0, n] - base, 0, TILES - 1)
        second = jnp.clip(pair_ref[1, n] - base, 0, 2 * TILES - 1)
        b = jnp.clip(bin_ref[n], 0, NBIN - 1)
        product(
            lambda rows: a_turned[TILES + first, rows, :], a_near[second], lambda rows: rho[b, rows, :], cov.at[n],
            cov_turned.at[n],
        )
        return 0


    @pl.when(not_first)
    def _():
        for copy in info_out + relays[0]:
            copy.wait_recv()

    base_before = lax.rem(me + size - 1, size) * TILES
    far = [(before_pair[0, n] - base_before, before_pair[1, n] - base_before, before_bin[n]) for n in range(SLOTS)]

    def turn(t, _):
        a_turned[t] = a_left[t].T
        return 0

    lax.fori_loop(0, TILES, turn, 0)

    def far_ends(n):
        first = jnp.clip(before_pair[0, n] - base_before, 0, TILES - 1)
        second = jnp.clip(before_pair[1, n] - base_before - TILES, TILES, 2 * TILES - 1)
        return first, second

    def far_covariance(n, _):
        first, second = far_ends(n)
        b = jnp.clip(before_bin[n], 0, NBIN - 1)
        product(
            lambda rows: a_turned[first, rows, :], a_near[second], lambda rows: rho[b, rows, :], cov.at[SLOTS + n],
            cov_turned.at[SLOTS + n],
        )
        return 0

    def covariances(n, _):
        near_covariance(n, 0)
        far_covariance(n, 0)
        return 0

    lax.fori_loop(0, SLOTS, covariances, 0, unroll=UNROLL)

    def near_seconds(n, _):
        first = jnp.clip(pair_ref[0, n] - base, 0, TILES - 1)
        near_second[n] = jnp.dot(g_own[first], cov[n], preferred_element_type=jnp.float32)
        return 0

    lax.fori_loop(0, SLOTS, near_seconds, 0, unroll=4)

    def share_of(alive, end, tile, b):
        return jnp.where(alive & (end == tile) & (b < NBIN), 1.0, 0.0).astype(jnp.float32)

    for h in range(CHUNKS):
        rows = slice(h * ROWS, (h + 1) * ROWS)
        for t in range(TILES):
            total = jnp.zeros((ROWS, POINTS), jnp.float32)
            for n, (_, second, b) in enumerate(near):
                total = total + share_of(second < 2 * TILES, second, TILES + t, b) * near_second[n, rows, :]
            right_sum[t, rows, :] = total

    i_out = [[], []]
    for h in range(CHUNKS):
        rows = slice(h * ROWS, (h + 1) * ROWS)
        for side in range(2):
            pl.when(from_side[side])(g_out[side][h].wait_recv)

        def increments(n, _):
            first, second = far_ends(n)
            far_first[n] = jnp.dot(g_near[h][second], cov_turned[SLOTS + n], preferred_element_type=jnp.float32)
            far_second[n] = jnp.dot(g_left[h][first], cov[SLOTS + n], preferred_element_type=jnp.float32)
            return 0

        lax.fori_loop(0, SLOTS, increments, 0, unroll=4)
        for t in range(TILES):
            to_left = jnp.zeros((ROWS, POINTS), jnp.float32)
            to_right = right_sum[t, rows, :]
            for n, (first, second, b) in enumerate(far):
                alive = second >= 2 * TILES
                to_left = to_left + share_of(alive, first, t, b) * far_first[n]
                to_right = to_right + share_of(alive, second, 2 * TILES + t, b) * far_second[n]
            i_left[h, t] = to_left.astype(jnp.bfloat16)
            i_right[h, t] = to_right.astype(jnp.bfloat16)
        for side, (device, src, dst) in enumerate(((right, i_right, from_left), (left, i_left, from_right))):
            i_out[side].append(send(src.at[h], dst.at[h], i_send.at[side, h], i_recv.at[side, h], device))
            pl.when(to_side[side])(i_out[side][h].start)

    for t in range(TILES):
        total = jnp.dot(g_own[t], own_cov[t], preferred_element_type=jnp.float32)
        own_sum[t] = total + a_near[t, mine, :].astype(jnp.float32)

    def near_increment(n, _):
        first = jnp.clip(pair_ref[0, n] - base, 0, TILES - 1)
        second = jnp.clip(pair_ref[1, n] - base, 0, 2 * TILES - 1)
        alive = (pair_ref[1, n] - base < 2 * TILES) & (bin_ref[n] < NBIN)
        forcing = jnp.concatenate([g_near[h][second] for h in range(CHUNKS)], axis=0)
        to_first = jnp.dot(forcing, cov_turned[n], preferred_element_type=jnp.float32)
        for t in range(TILES):
            share_first = jnp.where(alive & (first == t), 1.0, 0.0).astype(jnp.float32)
            share_second = jnp.where(alive & (second == t), 1.0, 0.0).astype(jnp.float32)
            own_sum[t] = own_sum[t] + (share_first * to_first + share_second * near_second[n])
        return 0

    lax.fori_loop(0, SLOTS, near_increment, 0)

    for h in range(CHUNKS):
        rows = slice(h * ROWS, (h + 1) * ROWS)
        for side in range(2):
            pl.when(from_side[side])(i_out[side][h].wait_recv)
        for t in range(TILES):
            total = own_sum[t, rows, :] + from_left[h, t].astype(jnp.float32) + from_right[h, t].astype(jnp.float32)
            out_ref[t, rows, :] = total.astype(jnp.bfloat16)

    for copy in a_out[2]:
        copy.wait_send()
    for side in range(2):

        @pl.when(to_side[side])
        def _():
            for copy in a_out[side] + g_out[side] + i_out[side]:
                copy.wait_send()

        @pl.when(from_side[side])
        def _():
            for copy in relays[side]:
                copy.wait_send()

    @pl.when(not_last)
    def _():
        for copy in info_out:
            copy.wait_send()


def hand_on(src, dst, sem):
    copy = pltpu.make_async_copy(src, dst, sem)
    copy.start()
    copy.wait()


def per_device(anomalies, innovations, obs_tile, pair_tiles, loc_bin):
    bf16, f32 = jnp.bfloat16, jnp.float32
    vmem, smem = pl.BlockSpec(memory_space=pltpu.VMEM), pl.BlockSpec(memory_space=pltpu.SMEM)
    hbm = pl.BlockSpec(memory_space=pl.ANY)
    dma = pltpu.SemaphoreType.DMA
    made = pl.pallas_call(
        kernel,
        name="analysis",
        out_shape=pltpu.VMEM(anomalies.shape, bf16),
        in_specs=[smem, smem, smem, hbm, hbm],
        out_specs=vmem,
        scratch_shapes=[
            pltpu.VMEM(innovations.shape, bf16),
            pltpu.SMEM((2, SLOTS), jnp.int32),
            pltpu.SMEM((SLOTS,), jnp.int32),
            pltpu.VMEM((TILES, MEMBERS, POINTS), bf16),
            pltpu.VMEM((2 * TILES, MEMBERS, POINTS), bf16),
            pltpu.VMEM((2 * TILES, POINTS, MEMBERS), bf16),
            pltpu.VMEM((TILES, HALF, POINTS), bf16),
            pltpu.VMEM((TILES, ROWS, POINTS), bf16),
            pltpu.VMEM((TILES, ROWS, POINTS), bf16),
            pltpu.VMEM((2 * TILES, ROWS, POINTS), bf16),
            pltpu.VMEM((2 * TILES, ROWS, POINTS), bf16),
            pltpu.VMEM((NBIN, POINTS, POINTS), f32),
            pltpu.VMEM((2 * SLOTS, POINTS, POINTS), bf16),
            pltpu.VMEM((2 * SLOTS, POINTS, POINTS), bf16),
            pltpu.VMEM((TILES, POINTS, POINTS), bf16),
            pltpu.VMEM((SLOTS, HALF, POINTS), f32),
            pltpu.VMEM((SLOTS, ROWS, POINTS), f32),
            pltpu.VMEM((SLOTS, ROWS, POINTS), f32),
            pltpu.VMEM((TILES, HALF, POINTS), f32),
            pltpu.VMEM((TILES, HALF, POINTS), f32),
            pltpu.VMEM((CHUNKS, TILES, ROWS, POINTS), bf16),
            pltpu.VMEM((CHUNKS, TILES, ROWS, POINTS), bf16),
            pltpu.VMEM((CHUNKS, TILES, ROWS, POINTS), bf16),
            pltpu.VMEM((CHUNKS, TILES, ROWS, POINTS), bf16),
            dma((3, TILES)), dma((3, TILES)),
            dma((2, TILES)), dma((2, TILES)),
            dma((2, CHUNKS)), dma((2, CHUNKS)),
            dma((2, CHUNKS)), dma((2, CHUNKS)),
            dma((2,)), dma((2,)), dma((2,)),
        ],
        compiler_params=pltpu.CompilerParams(collective_id=0, has_side_effects=True, vmem_limit_bytes=56 << 20),
    )(obs_tile, pair_tiles.T, loc_bin, anomalies, innovations)
    return pl.pallas_call(
        hand_on,
        name="hand_on",
        out_shape=jax.ShapeDtypeStruct(anomalies.shape, bf16),
        in_specs=[vmem],
        out_specs=hbm,
        scratch_shapes=[pltpu.SemaphoreType.DMA],
    )(pltpu.with_memory_space_constraint(made, pltpu.VMEM))


def solution(mesh):
    return jax.shard_map(
        per_device,
        mesh=mesh,
        in_specs=(
            P("tile", "mem", None),
            P("tile", "mem", None),
            P("tile"),
            P("tile", None),
            P("tile"),
        ),
        out_specs=P("tile", "mem", None),
        check_vma=False,
    )
```

```python
import functools

import jax
import jax.numpy as jnp
from jax import lax
from jax.experimental import pallas as pl
from jax.experimental.pallas import tpu as pltpu
from jax.sharding import PartitionSpec as P

MEMBERS = 256
POINTS = 512
NBIN = 4
RADIUS = 4
TILES = 4
SLOTS = 8
BLOCKS = 8
HALF = MEMBERS // 2
CHUNKS = 2
ROWS = HALF // CHUNKS
BAND = 128
UNROLL = 4
TALL = 256
MESH = pl.DeviceIdType.MESH


def kernel(
    obs_ref, pair_ref, bin_ref, a_ref, innov_hbm, out_ref,
    innov_ref, before_pair, before_bin, a_left, a_near, a_turned, g_own, g_left0, g_left1, g_near0, g_near1,
    rho, cov, cov_turned, own_cov, near_second, far_first, far_second,
    right_sum, own_sum, i_left, i_right, from_left, from_right,
    a_send, a_recv, relay_send, relay_recv, g_send, g_recv, i_send, i_recv, info_send, info_recv, load_sem,
):
    core = lax.axis_index("mem")
    me = lax.axis_index("tile")
    size = lax.axis_size("tile")
    right = (core, lax.rem(me + 1, size))
    left = (core, lax.rem(me + size - 1, size))
    sibling = (1 - core, me)
    g_left, g_near = (g_left0, g_left1), (g_near0, g_near1)

    def send(src, dst, send_sem, recv_sem, device):
        return pltpu.make_async_remote_copy(
            src_ref=src, dst_ref=dst, send_sem=send_sem, recv_sem=recv_sem, device_id=device, device_id_type=MESH
        )

    mine = pl.ds(pl.multiple_of(core * HALF, HALF), HALF)
    load_innov = pltpu.make_async_copy(innov_hbm, innov_ref, load_sem.at[0])
    load_a = pltpu.make_async_copy(a_ref, a_near.at[:TILES, mine], load_sem.at[1])
    load_innov.start()
    load_a.start()

    not_first, not_last = me > 0, me < size - 1
    to_side, from_side = (not_last, not_first), (not_first, not_last)

    barrier = pltpu.get_barrier_semaphore()
    for device, there in ((left, not_first), (right, not_last), (sibling, None)):

        def greet():
            pl.semaphore_signal(barrier, inc=1, device_id=device, device_id_type=MESH)

        greet() if there is None else pl.when(there)(greet)
    both = not_first & not_last

    @pl.when(both)
    def _():
        pl.semaphore_wait(barrier, 3)

    @pl.when(jnp.logical_not(both))
    def _():
        pl.semaphore_wait(barrier, 2)

    a_out = [[], [], []]
    for t in range(TILES):
        for side, (device, there) in enumerate(
            ((right, a_left.at[t, mine]), (left, a_near.at[TILES + t, mine]), (sibling, a_near.at[t, mine]))
        ):
            a_out[side].append(send(a_ref.at[t], there, a_send.at[side, t], a_recv.at[side, t], device))
    info_out = [
        send(pair_ref, before_pair, info_send.at[0], info_recv.at[0], right),
        send(bin_ref, before_bin, info_send.at[1], info_recv.at[1], right),
    ]
    for t in range(TILES):
        for side in range(2):
            pl.when(to_side[side])(a_out[side][t].start)
        a_out[2][t].start()

    @pl.when(not_last)
    def _():
        for copy in info_out:
            copy.start()

    @pl.when(me == 0)
    def _():
        a_left[...] = jnp.zeros_like(a_left)
        from_left[...] = jnp.zeros_like(from_left)
        for h in range(CHUNKS):
            g_left[h][...] = jnp.zeros_like(g_left[h])
        for n in range(SLOTS):
            before_bin[n] = NBIN
            before_pair[0, n] = 0
            before_pair[1, n] = 0

    @pl.when(me == size - 1)
    def _():
        a_near[TILES:] = jnp.zeros((TILES, MEMBERS, POINTS), jnp.bfloat16)
        from_right[...] = jnp.zeros_like(from_right)
        for h in range(CHUNKS):
            g_near[h][TILES:] = jnp.zeros((TILES, ROWS, POINTS), jnp.bfloat16)

    load_innov.wait()
    base = me * TILES
    g_out = [[], []]
    for h in range(CHUNKS):
        rows = slice(h * ROWS, (h + 1) * ROWS)
        for t in range(TILES):
            total = jnp.zeros((ROWS, POINTS), jnp.float32)
            for o in range(BLOCKS):
                share = jnp.where(obs_ref[o] - base == t, 1.0, 0.0).astype(jnp.float32)
                total = total + share * innov_ref[o, rows, :].astype(jnp.float32)
            g_own[t, rows, :] = total.astype(jnp.bfloat16)
            g_near[h][t] = total.astype(jnp.bfloat16)
        here = g_own.at[:, rows]
        for side, (device, there) in enumerate(((right, g_left[h]), (left, g_near[h].at[TILES:]))):
            g_out[side].append(send(here, there, g_send.at[side, h], g_recv.at[side, h], device))

    def weigh(n, _):
        b = n // (POINTS // BAND)
        start = pl.multiple_of(lax.rem(n, POINTS // BAND) * BAND, BAND)
        p = lax.broadcasted_iota(jnp.int32, (BAND, POINTS), 0) + start
        q = lax.broadcasted_iota(jnp.int32, (BAND, POINTS), 1)
        along = ((q & 31) - (p & 31)).astype(jnp.float32) + 0.5 * RADIUS * b.astype(jnp.float32)
        across = ((q >> 5) - (p >> 5)).astype(jnp.float32)
        weight = jnp.exp(-(along * along + across * across) / (2.0 * RADIUS * RADIUS))
        rho[b, pl.ds(start, BAND), :] = weight * (1.0 / (MEMBERS - 1))
        return 0

    lax.fori_loop(0, NBIN * (POINTS // BAND), weigh, 0)

    def product(turned, second, weights_of, target, also_turned=None):
        for band in range(POINTS // TALL):
            rows = slice(band * TALL, (band + 1) * TALL)
            cross = jnp.dot(turned(rows), second, preferred_element_type=jnp.float32)
            rounded = (weights_of(rows) * cross).astype(jnp.bfloat16)
            target[rows, :] = rounded
            if also_turned is not None:
                also_turned[:, rows] = rounded.T

    load_a.wait()
    for t in range(TILES):
        a_out[2][t].wait_recv()

    def own_product(t, _):
        tile = a_near[t]
        a_turned[TILES + t] = tile.T
        product(lambda rows: a_turned[TILES + t, rows, :], tile, lambda rows: rho[0, rows, :], own_cov.at[t])
        return 0

    lax.fori_loop(0, TILES, own_product, 0)

    relays = [[], []]
    for t in range(TILES):
        for side, here in ((0, a_left.at[t, mine]), (1, a_near.at[TILES + t, mine])):
            relays[side].append(send(here, here, relay_send.at[side, t], relay_recv.at[side, t], sibling))

            @pl.when(from_side[side])
            def _():
                a_out[side][t].wait_recv()
                relays[side][t].start()

        if t >= TILES - 2:
            for side in range(2):
                pl.when(to_side[side])(g_out[side][t - TILES + 2].start)


    @pl.when(not_last)
    def _():
        for copy in relays[1]:
            copy.wait_recv()

    near = [(pair_ref[0, n] - base, pair_ref[1, n] - base, bin_ref[n]) for n in range(SLOTS)]

    def near_covariance(n, _):
        first = jnp.clip(pair_ref[0, n] - base, 0, TILES - 1)
        second = jnp.clip(pair_ref[1, n] - base, 0, 2 * TILES - 1)
        b = jnp.clip(bin_ref[n], 0, NBIN - 1)
        product(
            lambda rows: a_turned[TILES + first, rows, :], a_near[second], lambda rows: rho[b, rows, :], cov.at[n],
            cov_turned.at[n],
        )
        return 0


    @pl.when(not_first)
    def _():
        for copy in info_out + relays[0]:
            copy.wait_recv()

    base_before = lax.rem(me + size - 1, size) * TILES
    far = [(before_pair[0, n] - base_before, before_pair[1, n] - base_before, before_bin[n]) for n in range(SLOTS)]

    def turn(t, _):
        a_turned[t] = a_left[t].T
        return 0

    lax.fori_loop(0, TILES, turn, 0, unroll=4)

    def far_ends(n):
        first = jnp.clip(before_pair[0, n] - base_before, 0, TILES - 1)
        second = jnp.clip(before_pair[1, n] - base_before - TILES, TILES, 2 * TILES - 1)
        return first, second

    def far_covariance(n, _):
        first, second = far_ends(n)
        b = jnp.clip(before_bin[n], 0, NBIN - 1)
        product(
            lambda rows: a_turned[first, rows, :], a_near[second], lambda rows: rho[b, rows, :], cov.at[SLOTS + n],
            cov_turned.at[SLOTS + n],
        )
        return 0

    def covariances(n, _):
        near_covariance(n, 0)
        far_covariance(n, 0)
        return 0

    lax.fori_loop(0, SLOTS, covariances, 0, unroll=UNROLL)

    def near_seconds(n, _):
        first = jnp.clip(pair_ref[0, n] - base, 0, TILES - 1)
        near_second[n] = jnp.dot(g_own[first], cov[n], preferred_element_type=jnp.float32)
        return 0

    lax.fori_loop(0, SLOTS, near_seconds, 0, unroll=8)

    def share_of(alive, end, tile, b):
        return jnp.where(alive & (end == tile) & (b < NBIN), 1.0, 0.0).astype(jnp.float32)

    for h in range(CHUNKS):
        rows = slice(h * ROWS, (h + 1) * ROWS)
        for t in range(TILES):
            total = jnp.zeros((ROWS, POINTS), jnp.float32)
            for n, (_, second, b) in enumerate(near):
                total = total + share_of(second < 2 * TILES, second, TILES + t, b) * near_second[n, rows, :]
            right_sum[t, rows, :] = total

    i_out = [[], []]
    for h in range(CHUNKS):
        rows = slice(h * ROWS, (h + 1) * ROWS)
        for side in range(2):
            pl.when(from_side[side])(g_out[side][h].wait_recv)

        def increments(n, _):
            first, second = far_ends(n)
            far_first[n] = jnp.dot(g_near[h][second], cov_turned[SLOTS + n], preferred_element_type=jnp.float32)
            far_second[n] = jnp.dot(g_left[h][first], cov[SLOTS + n], preferred_element_type=jnp.float32)
            return 0

        lax.fori_loop(0, SLOTS, increments, 0, unroll=8)
        for t in range(TILES):
            to_left = jnp.zeros((ROWS, POINTS), jnp.float32)
            to_right = right_sum[t, rows, :]
            for n, (first, second, b) in enumerate(far):
                alive = second >= 2 * TILES
                to_left = to_left + share_of(alive, first, t, b) * far_first[n]
                to_right = to_right + share_of(alive, second, 2 * TILES + t, b) * far_second[n]
            i_left[h, t] = to_left.astype(jnp.bfloat16)
            i_right[h, t] = to_right.astype(jnp.bfloat16)
        for side, (device, src, dst) in enumerate(((right, i_right, from_left), (left, i_left, from_right))):
            i_out[side].append(send(src.at[h], dst.at[h], i_send.at[side, h], i_recv.at[side, h], device))
            pl.when(to_side[side])(i_out[side][h].start)

    for t in range(TILES):
        total = jnp.dot(g_own[t], own_cov[t], preferred_element_type=jnp.float32)
        own_sum[t] = total + a_near[t, mine, :].astype(jnp.float32)

    def near_increment(n, _):
        first = jnp.clip(pair_ref[0, n] - base, 0, TILES - 1)
        second = jnp.clip(pair_ref[1, n] - base, 0, 2 * TILES - 1)
        alive = (pair_ref[1, n] - base < 2 * TILES) & (bin_ref[n] < NBIN)
        forcing = jnp.concatenate([g_near[h][second] for h in range(CHUNKS)], axis=0)
        to_first = jnp.dot(forcing, cov_turned[n], preferred_element_type=jnp.float32)
        for t in range(TILES):
            share_first = jnp.where(alive & (first == t), 1.0, 0.0).astype(jnp.float32)
            share_second = jnp.where(alive & (second == t), 1.0, 0.0).astype(jnp.float32)
            own_sum[t] = own_sum[t] + (share_first * to_first + share_second * near_second[n])
        return 0

    lax.fori_loop(0, SLOTS, near_increment, 0)

    for h in range(CHUNKS):
        rows = slice(h * ROWS, (h + 1) * ROWS)
        for side in range(2):
            pl.when(from_side[side])(i_out[side][h].wait_recv)
        for t in range(TILES):
            total = own_sum[t, rows, :] + from_left[h, t].astype(jnp.float32) + from_right[h, t].astype(jnp.float32)
            out_ref[t, rows, :] = total.astype(jnp.bfloat16)

    for copy in a_out[2]:
        copy.wait_send()
    for side in range(2):

        @pl.when(to_side[side])
        def _():
            for copy in a_out[side] + g_out[side] + i_out[side]:
                copy.wait_send()

        @pl.when(from_side[side])
        def _():
            for copy in relays[side]:
                copy.wait_send()

    @pl.when(not_last)
    def _():
        for copy in info_out:
            copy.wait_send()


def hand_on(src, dst, sem):
    copy = pltpu.make_async_copy(src, dst, sem)
    copy.start()
    copy.wait()


def per_device(anomalies, innovations, obs_tile, pair_tiles, loc_bin):
    bf16, f32 = jnp.bfloat16, jnp.float32
    vmem, smem = pl.BlockSpec(memory_space=pltpu.VMEM), pl.BlockSpec(memory_space=pltpu.SMEM)
    hbm = pl.BlockSpec(memory_space=pl.ANY)
    dma = pltpu.SemaphoreType.DMA
    made = pl.pallas_call(
        kernel,
        name="analysis",
        out_shape=pltpu.VMEM(anomalies.shape, bf16),
        in_specs=[smem, smem, smem, hbm, hbm],
        out_specs=vmem,
        scratch_shapes=[
            pltpu.VMEM(innovations.shape, bf16),
            pltpu.SMEM((2, SLOTS), jnp.int32),
            pltpu.SMEM((SLOTS,), jnp.int32),
            pltpu.VMEM((TILES, MEMBERS, POINTS), bf16),
            pltpu.VMEM((2 * TILES, MEMBERS, POINTS), bf16),
            pltpu.VMEM((2 * TILES, POINTS, MEMBERS), bf16),
            pltpu.VMEM((TILES, HALF, POINTS), bf16),
            pltpu.VMEM((TILES, ROWS, POINTS), bf16),
            pltpu.VMEM((TILES, ROWS, POINTS), bf16),
            pltpu.VMEM((2 * TILES, ROWS, POINTS), bf16),
            pltpu.VMEM((2 * TILES, ROWS, POINTS), bf16),
            pltpu.VMEM((NBIN, POINTS, POINTS), f32),
            pltpu.VMEM((2 * SLOTS, POINTS, POINTS), bf16),
            pltpu.VMEM((2 * SLOTS, POINTS, POINTS), bf16),
            pltpu.VMEM((TILES, POINTS, POINTS), bf16),
            pltpu.VMEM((SLOTS, HALF, POINTS), f32),
            pltpu.VMEM((SLOTS, ROWS, POINTS), f32),
            pltpu.VMEM((SLOTS, ROWS, POINTS), f32),
            pltpu.VMEM((TILES, HALF, POINTS), f32),
            pltpu.VMEM((TILES, HALF, POINTS), f32),
            pltpu.VMEM((CHUNKS, TILES, ROWS, POINTS), bf16),
            pltpu.VMEM((CHUNKS, TILES, ROWS, POINTS), bf16),
            pltpu.VMEM((CHUNKS, TILES, ROWS, POINTS), bf16),
            pltpu.VMEM((CHUNKS, TILES, ROWS, POINTS), bf16),
            dma((3, TILES)), dma((3, TILES)),
            dma((2, TILES)), dma((2, TILES)),
            dma((2, CHUNKS)), dma((2, CHUNKS)),
            dma((2, CHUNKS)), dma((2, CHUNKS)),
            dma((2,)), dma((2,)), dma((2,)),
        ],
        compiler_params=pltpu.CompilerParams(collective_id=0, has_side_effects=True, vmem_limit_bytes=56 << 20),
    )(obs_tile, pair_tiles.T, loc_bin, anomalies, innovations)
    return pl.pallas_call(
        hand_on,
        name="hand_on",
        out_shape=jax.ShapeDtypeStruct(anomalies.shape, bf16),
        in_specs=[vmem],
        out_specs=hbm,
        scratch_shapes=[pltpu.SemaphoreType.DMA],
    )(pltpu.with_memory_space_constraint(made, pltpu.VMEM))


def solution(mesh):
    return jax.shard_map(
        per_device,
        mesh=mesh,
        in_specs=(
            P("tile", "mem", None),
            P("tile", "mem", None),
            P("tile"),
            P("tile", None),
            P("tile"),
        ),
        out_specs=P("tile", "mem", None),
        check_vma=False,
    )
```
